32 devices in a mesh: dp: 2 (over x), ctx: 16 (over z, y, core).
Axes of the slice: x: 2, y: 2, z: 4, core: 2. Of those that a mesh axis runs over, the one named last changes fastest.
Arguments:
- queries: bfloat16 [32, 4096, 128], P(None, ('dp', 'ctx')), parts along dimension 1, may hold values from -150 to 150
- query_pos: bfloat16 [32, 4096, 64], P(None, ('dp', 'ctx')), parts along dimension 1, may hold values from -300 to 300
- key_values: bfloat16 [4, 2, 4096, 128], P(None, None, ('dp', 'ctx')), parts along dimension 2, may hold values from -20 to 20
- latent: bfloat16 [4096, 512], P(('dp', 'ctx')), parts along dimension 0, may hold values from -6 to 6
- key_pos: bfloat16 [4096, 64], P(('dp', 'ctx')), parts along dimension 0, may hold values from -4 to 4
- key_upward_matrix: bfloat16 [32, 128, 512], P(None, None, 'ctx'), may hold values from -0.5 to 0.5
- value_upward_matrix: bfloat16 [32, 512, 128], P(None, 'ctx'), may hold values from -1 to 1
- segment_ids: int32 [4096], P(('dp', 'ctx')), parts along dimension 0, may hold values from 0 to 15, never falling along the last dimension, each value on 1 to 256 neighbouring positions
Outputs:
- student_out: bfloat16 [32, 4096, 128], P(None, ('dp', 'ctx')), parts along dimension 1
- token_error: float32 [4096], P(('dp', 'ctx')), parts along dimension 0
The draws below stay inside these ranges and needn't reach their ends.
There are 2 independent parts, one for each index of `dp`. The reference program is written for one: setup_inputs(seed, part) draws one part's arguments, and reference() takes and returns one part's arrays. A program takes and returns all parts, laid end to end along the dimension named above; an argument that names none is the same for every part. Nothing has to cross between parts.
Inputs may be any that keep to these rules, and one draw needn't show every extreme that they name: `segment_ids`: each document covers at most 256 consecutive positions; ids never fall along the sequence.
All inputs are finite; a program needn't handle non-finite values.
Results may differ from the reference program's by a relative error of at most 0.0071.
Values may be sent and summed in bfloat16 or wider, within the bound.
A program may use at most 64 MiB of HBM per device.

```python
import math
import jax
import jax.numpy as jnp
import numpy as np
from jax import lax

HEADS = 32
KV_HEADS = 4
HEAD_DIM = 128
LATENT = 512
ROPE_DIM = 64
TOK_DEV = 128
REACH = 2
TOKENS = 2048
DOC_MOST = 256
DOCS = 16


def joint_draw(key):
    base = jax.random.fold_in(key, 11)
    streams = jax.random.split(base, 4)
    queries = jnp.clip(jax.random.normal(streams[0], (HEADS, TOKENS, HEAD_DIM), jnp.float32), -5.0, 5.0)
    pair = jnp.clip(jax.random.normal(streams[1], (KV_HEADS, 2, TOKENS, HEAD_DIM), jnp.float32), -5.0, 5.0)
    pair = pair * jnp.array([1.0, 4.0], jnp.float32).reshape(1, 2, 1, 1)
    query_pos = jnp.clip(jax.random.normal(streams[2], (HEADS, TOKENS, ROPE_DIM), jnp.float32), -4.0, 4.0)
    key_pos = jnp.clip(jax.random.normal(streams[3], (TOKENS, ROPE_DIM), jnp.float32), -4.0, 4.0)
    return (queries, pair, query_pos, key_pos)


def draw_queries(key, part):
    return joint_draw(key)[0].astype(jnp.bfloat16)


def draw_key_values(key, part):
    return joint_draw(key)[1].astype(jnp.bfloat16)


def draw_query_pos(key, part):
    return joint_draw(key)[2].astype(jnp.bfloat16)


def draw_key_pos(key, part):
    return joint_draw(key)[3].astype(jnp.bfloat16)


def levels(rng, extent, cuts, smallest, high):
    factor_of = 1.0
    for position, blocks in cuts:
        draws = jax.random.uniform(jax.random.fold_in(jax.random.fold_in(rng, 6), position), (blocks,), jnp.float32, smallest / len(cuts), high / len(cuts))
        factor_of = factor_of * jnp.repeat(jnp.exp(draws), extent[position] // blocks).reshape((-1,) + (1,) * (len(extent) - 1 - position))
    return factor_of


def length_profile(count, total, most, slope):
    portions = [(1 << 20) // math.isqrt(rank ** slope) + 1 for rank in range(2, count + 1)]
    surplus, holding = total - most - (count - 1), [1] * (count - 1)
    while surplus > 0:
        candidates = [i for i in range(count - 1) if holding[i] < most]
        pool, remaining = sum([portions[i] for i in candidates]), surplus
        for i in candidates:
            more = min(most - holding[i], max(1, remaining * portions[i] // pool), surplus)
            holding[i] = holding[i] + more
            surplus = surplus - more
    return np.array([most] + holding)


def uneven_parts(own_key, number_of, total, most, skew):
    if number_of == 2:
        one = jax.random.randint(own_key, (), max(1, total - most), min(most, total - 1) + 1)
        return jnp.stack([one, total - one])
    lengths = jnp.asarray(length_profile(number_of, total, most, skew), jnp.int32)
    couples = (number_of - 1) // 2
    source_of, sink = lengths[1:1 + 2 * couples:2], lengths[2:2 + 2 * couples:2]
    room = jnp.minimum(source_of - 1, most - sink)
    passed = jax.random.randint(jax.random.fold_in(own_key, 1), (couples,), 0, 1 << 20) % (room + 1)
    lengths = lengths.at[1:1 + 2 * couples:2].set(source_of - passed).at[2:2 + 2 * couples:2].set(sink + passed)
    return lengths[jax.random.permutation(jax.random.fold_in(own_key, 2), number_of)]


def normal_values(own_key, dims, deviation, most, cuts=(), kind=jnp.bfloat16):
    level = levels(own_key, dims, cuts, -0.22, 0.18) if cuts else 1.0
    entries = jax.random.normal(own_key, dims, jnp.float32) * deviation * level
    return jnp.minimum(jnp.maximum(entries, -most), most).astype(kind)


def setup_inputs(seed: int = 0, part: int = 0) -> dict:
    key_list = jax.random.split(jax.random.key(seed), 9)
    part_splits = jax.random.split(jax.random.fold_in(key_list[8], part), 9)
    return {
        "queries": draw_queries(jax.random.fold_in(jax.random.fold_in(key_list[8], part), 71), part),
        "query_pos": draw_query_pos(jax.random.fold_in(jax.random.fold_in(key_list[8], part), 71), part),
        "key_values": draw_key_values(jax.random.fold_in(jax.random.fold_in(key_list[8], part), 71), part),
        "latent": normal_values(part_splits[3], (TOKENS, LATENT), 1.0, 6.0, ((0, 16),)),
        "key_pos": draw_key_pos(jax.random.fold_in(jax.random.fold_in(key_list[8], part), 71), part),
        "key_upward_matrix": normal_values(key_list[5], (HEADS, HEAD_DIM, LATENT), HEAD_DIM ** -0.5, 0.5, ((2, 16),)),
        "value_upward_matrix": normal_values(key_list[6], (HEADS, LATENT, HEAD_DIM), (LATENT // 16) ** -0.5, 1.0, ((1, 16),)),
        "segment_ids": jnp.searchsorted(jnp.cumsum(uneven_parts(part_splits[7], DOCS, TOKENS, DOC_MOST, 2)), jnp.arange(TOKENS), side="right").astype(jnp.int32),
    }


def masked_softmax(scores, allowed):
    scores = jnp.where(allowed, scores, -jnp.inf)
    highest = lax.optimization_barrier(jnp.max(scores, axis=-1, keepdims=True))
    raised = jnp.exp(scores - highest)
    return raised / lax.optimization_barrier(jnp.sum(raised, axis=-1, keepdims=True))

def reference(queries, query_pos, key_values, latent, key_pos, key_upward_matrix, value_upward_matrix, segment_ids):
    reach_len = REACH * TOK_DEV
    window = reach_len + TOK_DEV
    groups = HEADS // KV_HEADS
    pair_padded = jnp.pad(key_values, ((0, 0), (0, 0), (reach_len, 0), (0, 0)))
    latent_padded = jnp.pad(latent, ((reach_len, 0), (0, 0)))
    pos_padded = jnp.pad(key_pos, ((reach_len, 0), (0, 0)))
    seg_padded = jnp.pad(segment_ids, (reach_len, 0))
    teacher_scale = 1.0 / math.sqrt(HEAD_DIM)
    student_scale = 1.0 / math.sqrt(HEAD_DIM + ROPE_DIM)
    keys_up = key_upward_matrix.astype(jnp.float32)
    values_up = value_upward_matrix.astype(jnp.float32)

    def one_block(block_id):
        first_row = (block_id * TOK_DEV).astype(jnp.int32)
        query_index = first_row + jnp.arange(TOK_DEV, dtype=jnp.int32)
        key_index = first_row - reach_len + jnp.arange(window, dtype=jnp.int32)
        query_seg = lax.dynamic_slice_in_dim(segment_ids, first_row, TOK_DEV, 0)
        key_seg = lax.dynamic_slice_in_dim(seg_padded, first_row, window, 0)
        allowed = (key_seg[None, :] == query_seg[:, None]) & (key_index[None, :] <= query_index[:, None]) & (key_index[None, :] >= 0)
        current_query_block = lax.dynamic_slice_in_dim(queries, first_row, TOK_DEV, 1).astype(jnp.float32)
        qpos_block = lax.dynamic_slice_in_dim(query_pos, first_row, TOK_DEV, 1).astype(jnp.float32)
        pair_block = lax.dynamic_slice_in_dim(pair_padded, first_row, window, 2).astype(jnp.float32)
        grouped = current_query_block.reshape(KV_HEADS, groups, TOK_DEV, HEAD_DIM)
        teacher_scores = jnp.einsum('kgtd,kld->kgtl', grouped, pair_block[:, 0]) * teacher_scale
        teacher_weights = masked_softmax(teacher_scores, allowed[None, None]).astype(jnp.bfloat16)
        teacher_out = jnp.einsum('kgtl,kld->kgtd', teacher_weights.astype(jnp.float32), pair_block[:, 1])
        teacher_out = teacher_out.astype(jnp.bfloat16).reshape(HEADS, TOK_DEV, HEAD_DIM)
        query_latent = jnp.einsum('htd,hdc->htc', current_query_block, keys_up).astype(jnp.bfloat16)
        latent_block = lax.dynamic_slice_in_dim(latent_padded, first_row, window, 0).astype(jnp.float32)
        kpos_block = lax.dynamic_slice_in_dim(pos_padded, first_row, window, 0).astype(jnp.float32)
        student_scores = jnp.einsum('htc,lc->htl', query_latent.astype(jnp.float32), latent_block)
        student_scores = (student_scores + jnp.einsum('htp,lp->htl', qpos_block, kpos_block)) * student_scale
        student_weights = masked_softmax(student_scores, allowed[None]).astype(jnp.bfloat16)
        latent_out = jnp.einsum('htl,lc->htc', student_weights.astype(jnp.float32), latent_block).astype(jnp.bfloat16)
        student_out = jnp.einsum('htc,hcd->htd', latent_out.astype(jnp.float32), values_up).astype(jnp.bfloat16)
        return (student_out, teacher_out)
    students, teachers = lax.map(one_block, jnp.arange(TOKENS // TOK_DEV, dtype=jnp.int32))
    student_out = jnp.transpose(students, (1, 0, 2, 3)).reshape(HEADS, TOKENS, HEAD_DIM)
    teacher_out = jnp.transpose(teachers, (1, 0, 2, 3)).reshape(HEADS, TOKENS, HEAD_DIM)
    difference = student_out.astype(jnp.float32) - teacher_out.astype(jnp.float32)
    token_error = lax.optimization_barrier(jnp.mean(difference * difference, axis=(0, 2)))
    return (student_out, token_error)
```

```python
import functools
import math

import jax
import jax.numpy as jnp
from jax import lax
from jax.experimental import pallas as pl
from jax.experimental.pallas import tpu as pltpu
from jax.sharding import PartitionSpec as P

REACH = 2
MASKED = -1e30
CHUNK = 2
LOG2E = 1.4426950408889634


def dot(a, b, dims):
    return lax.dot_general(a, b, (dims, ((), ())), preferred_element_type=jnp.float32)


def kernel(
    n,
    q_ref, qp_ref, kv_ref, lat_ref, kp_ref, ku_ref, vu_ref, seg_ref,
    out_ref, err_ref,
    G, QB, QPB, LATB, KPB, KVB, SEGB, BIAS, TO, SO, ACC, EROW, EIN,
    lsem, psend, precv, qsend, qrecv, hsend, hrecv, ssend, srecv,
    zs, zr, ys, yr, xs, xr, osend, orecv, olsem, esend, erecv, elsem,
):
    H, T, D = q_ref.shape
    C = lat_ref.shape[1]
    PD = qp_ref.shape[1]
    KV = kv_ref.shape[0]
    w = ku_ref.shape[1]
    Hh, KVh = H // 2, KV // 2
    hc = CHUNK
    nch = Hh // hc
    per_group = (H // KV) // hc
    Z = n // 4
    i = lax.axis_index("ctx")
    d = lax.axis_index("dp")
    k = i % 2
    y = (i // 2) % 2
    z = i // 4
    x = d % 2
    sib = i + 1 - 2 * k
    ynb = i + 2 - 4 * y
    dx = d + 1 - 2 * x
    pair = i // 2
    has_prev = pair > 0
    has_next = pair < n // 2 - 1
    has_up = z < Z - 1
    has_dn = z > 0

    def at(c, dd=d):
        return {"dp": dd, "ctx": c}

    def rc(src, dst, ss, rs, dev):
        return pltpu.make_async_remote_copy(
            src_ref=src, dst_ref=dst, send_sem=ss, recv_sem=rs,
            device_id=dev, device_id_type=pl.DeviceIdType.MESH)

    bar = pltpu.get_barrier_semaphore()

    def greet(dev):
        pl.semaphore_signal(bar, inc=1, device_id=dev, device_id_type=pl.DeviceIdType.MESH)

    def one_if(c):
        return jnp.where(c, 1, 0).astype(jnp.int32)

    greet(at(sib))
    greet(at(ynb))
    greet(at(i, dx))

    @pl.when(has_up)
    def _():
        greet(at(i + 4))

    @pl.when(has_dn)
    def _():
        greet(at(i - 4))

    @pl.when(has_next)
    def _():
        greet(at(2 * pair + 2))
        greet(at(2 * pair + 3))

    @pl.when(has_prev)
    def _():
        greet(at(2 * pair - 2))
        greet(at(2 * pair - 1))

    mine = pl.ds(k * Hh, Hh)
    theirs = pl.ds((1 - k) * Hh, Hh)
    kmine = pl.ds(k * KVh, KVh)
    ktheirs = pl.ds((1 - k) * KVh, KVh)
    tl = pl.ds(pl.multiple_of((2 + k) * T, T), T)
    locals_ = [
        pltpu.make_async_copy(ku_ref.at[mine], G.at[i, 0], lsem.at[0]),
        pltpu.make_async_copy(vu_ref.at[mine], G.at[i, 1], lsem.at[1]),
        pltpu.make_async_copy(q_ref.at[mine], QB.at[k], lsem.at[2]),
        pltpu.make_async_copy(qp_ref.at[mine], QPB.at[k], lsem.at[3]),
        pltpu.make_async_copy(lat_ref, LATB.at[tl], lsem.at[4]),
        pltpu.make_async_copy(kp_ref, KPB.at[:, tl], lsem.at[5]),
        pltpu.make_async_copy(kv_ref.at[kmine], KVB.at[2 + k], lsem.at[6]),
        pltpu.make_async_copy(seg_ref, SEGB.at[2 + k], lsem.at[7]),
    ]
    for c in locals_:
        c.start()

    @pl.when(jnp.logical_not(has_prev))
    def _():
        LATB[0:2 * T] = jnp.zeros((2 * T, C), LATB.dtype)
        KPB[:, 0:2 * T] = jnp.zeros((PD, 2 * T), KPB.dtype)
        KVB[0:2] = jnp.zeros((2, KVh, 2, T, D), KVB.dtype)
        SEGB[0:2] = jnp.full((2, 1, T), -1, jnp.int32)

    pl.semaphore_wait(
        bar, 3 + one_if(has_up) + one_if(has_dn) + 2 * one_if(has_next) + 2 * one_if(has_prev))

    def p_copy(m, j):
        src = (ku_ref, vu_ref)[m]
        return rc(src.at[pl.ds((1 - k) * Hh + j * hc, hc)], G.at[i, m, pl.ds(j * hc, hc)],
                  psend.at[m, j], precv.at[m, j], at(sib))

    def p_wait(m, j):
        here = G.at[sib, m, pl.ds(j * hc, hc)]
        rc(here, here, psend.at[m, j], precv.at[m, j], at(sib)).wait_recv()

    def bundle(row, target, who, kh):
        col = pl.ds(pl.multiple_of(row * T, T), T)
        return [
            rc(lat_ref, LATB.at[col], hsend.at[who, 0], hrecv.at[row, 0], target),
            rc(kp_ref, KPB.at[:, col], hsend.at[who, 1], hrecv.at[row, 1], target),
            rc(kv_ref.at[kh], KVB.at[row], hsend.at[who, 2], hrecv.at[row, 2], target),
            rc(seg_ref, SEGB.at[row], hsend.at[who, 3], hrecv.at[row, 3], target),
        ]

    def bundle_wait(row):
        col = pl.ds(pl.multiple_of(row * T, T), T)
        for idx, ref in enumerate((LATB.at[col], KPB.at[:, col], KVB.at[row], SEGB.at[row])):
            rc(ref, ref, hsend.at[0, idx], hrecv.at[row, idx], at(sib)).wait_recv()

    q_copies = [
        rc(q_ref.at[theirs], QB.at[k], qsend.at[0], qrecv.at[0], at(sib)),
        rc(qp_ref.at[theirs], QPB.at[k], qsend.at[1], qrecv.at[1], at(sib)),
    ]
    for j in range(nch):
        for m in range(2):
            p_copy(m, j).start()
        if j == 0:
            for c in bundle(2 + k, at(sib), 0, ktheirs) + q_copies:
                c.start()

            @pl.when(has_next)
            def _():
                for t in range(2):
                    for c in bundle(k, at(2 * pair + 2 + t), 1 + t, pl.ds(t * KVh, KVh)):
                        c.start()

    for c in locals_[:2]:
        c.wait()

    def zpair(j, zz):
        return G.at[pl.ds(4 * zz + 2 * y, 2), :, pl.ds(j * hc, hc)]

    def single(j, zz, yy, xx):
        return G.at[4 * zz + 2 * yy + xx, :, pl.ds(j * hc, hc)]

    def up(j, zz):
        return rc(zpair(j, zz), zpair(j, zz), zs.at[0, j, zz], zr.at[j, zz], at(i + 4))

    def dn(j, zz):
        return rc(zpair(j, zz), zpair(j, zz), zs.at[1, j, zz], zr.at[j, zz], at(i - 4))

    def yc(j, zz):
        s = single(j, zz, y, x)
        return rc(s, s, ys.at[j, zz], yr.at[j, zz], at(ynb))

    def yc_wait(j, zz):
        s = single(j, zz, 1 - y, x)
        rc(s, s, ys.at[j, zz], yr.at[j, zz], at(ynb)).wait_recv()

    def xc(j, zz):
        s = single(j, zz, 1 - y, x)
        return rc(s, s, xs.at[j, zz], xr.at[j, zz], at(i, dx))

    def xc_wait(j, zz):
        s = single(j, zz, 1 - y, 1 - x)
        rc(s, s, xs.at[j, zz], xr.at[j, zz], at(i, dx)).wait_recv()

    def e1(j):
        for m in range(2):
            p_wait(m, j)

        @pl.when(has_up)
        def _():
            up(j, z).start()

        @pl.when(has_dn)
        def _():
            dn(j, z).start()

        yc(j, z).start()

    def e2(j, r):
        @pl.when(z - r >= 0)
        def _():
            zz = z - r
            up(j, zz).wait_recv()

            @pl.when(has_up)
            def _():
                up(j, zz).start()

            yc(j, zz).start()

        @pl.when(z + r < Z)
        def _():
            zz = z + r
            dn(j, zz).wait_recv()

            @pl.when(has_dn)
            def _():
                dn(j, zz).start()

            yc(j, zz).start()

    def e3(j, r):
        if r == 0:
            yc_wait(j, z)
            xc(j, z).start()
            return
        for sign in (-1, 1):
            zz = z + sign * r

            @pl.when((zz >= 0) & (zz < Z))
            def _():
                yc_wait(j, zz)
                xc(j, zz).start()

    def e4(j):
        for zz in range(Z):
            xc_wait(j, zz)

    def probs(s, pb, scale):
        rows = s.shape[0]
        s = (s.reshape(rows // T, T, 3 * T) + BIAS[pb][None]).reshape(rows, 3 * T)
        top = jnp.max(s, axis=-1, keepdims=True)
        e = jnp.exp2((s - top) * (scale * LOG2E))
        return e.astype(jnp.bfloat16), 1.0 / jnp.sum(e, axis=-1, keepdims=True)

    def teacher(j):
        heads = pl.ds(j * hc, hc)
        g = j // per_group
        for pb in range(2):
            q = QB[pb, heads].reshape(hc * T, D)
            keys = KVB[pb:pb + 3, g, 0].reshape(3 * T, D)
            vals = KVB[pb:pb + 3, g, 1].reshape(3 * T, D)
            e, inv = probs(dot(q, keys, ((1,), (1,))), pb, 1.0 / math.sqrt(D))
            o = dot(e, vals, ((1,), (0,))) * inv
            TO[pb, heads] = o.astype(jnp.bfloat16).reshape(hc, T, D)

    def student(j):
        qls = []
        for u in range(hc):
            h = j * hc + u
            q = QB[:, h].reshape(2 * T, D)
            up_k = G[:, 0, h].reshape(C, D)
            qls.append(dot(q, up_k, ((1,), (1,))).astype(jnp.bfloat16))
        los, invs = [], []
        for pb in range(2):
            rows = slice(pb * T, pb * T + 3 * T)
            lat = LATB[rows]
            kp = KPB[:, rows]
            ql = jnp.concatenate([a[pb * T:(pb + 1) * T] for a in qls], 0)
            pos = jnp.concatenate(
                [dot(QPB[pb, j * hc + u], kp, ((0,), (0,))) for u in range(hc)], 0)
            s = dot(ql, lat, ((1,), (1,))) + pos
            e, inv = probs(s, pb, 1.0 / math.sqrt(D + PD))
            los.append(dot(e, lat, ((1,), (0,))).astype(jnp.bfloat16))
            invs.append(inv)
        for u in range(hc):
            h = j * hc + u
            up_v = G[:, 1, h].reshape(C, D)
            cut = slice(u * T, (u + 1) * T)
            lo = jnp.concatenate([los[0][cut], los[1][cut]], 0)
            inv = jnp.concatenate([invs[0][cut], invs[1][cut]], 0)
            so = (dot(lo, up_v, ((1,), (0,))) * inv).astype(jnp.bfloat16).reshape(2, T, D)
            SO[:, h] = so
            diff = so.astype(jnp.float32) - TO[:, h].astype(jnp.float32)
            ACC[...] += diff * diff

    def o_remote(j):
        return rc(SO.at[1 - k, pl.ds(j * hc, hc)], out_ref.at[pl.ds(k * Hh + j * hc, hc)],
                  osend.at[j], orecv.at[j], at(sib))

    def o_wait(j):
        here = out_ref.at[pl.ds((1 - k) * Hh + j * hc, hc)]
        rc(here, here, osend.at[j], orecv.at[j], at(sib)).wait_recv()

    def o_local(j):
        return pltpu.make_async_copy(
            SO.at[k, pl.ds(j * hc, hc)], out_ref.at[pl.ds(k * Hh + j * hc, hc)], olsem.at[j])

    def prepare():
        for c in locals_[2:]:
            c.wait()
        for idx, ref in enumerate((QB.at[1 - k], QPB.at[1 - k])):
            rc(ref, ref, qsend.at[idx], qrecv.at[idx], at(sib)).wait_recv()
        bundle_wait(3 - k)

        @pl.when(has_prev)
        def _():
            bundle_wait(0)
            bundle_wait(1)

        ACC[...] = jnp.zeros_like(ACC)
        row = lax.broadcasted_iota(jnp.int32, (T, T), 0)
        lane = lax.broadcasted_iota(jnp.int32, (T, T), 1)
        for pb in range(2):
            own = jnp.transpose(jnp.broadcast_to(SEGB[2 + pb], (T, T)))
            for b in range(3):
                ok = jnp.broadcast_to(SEGB[pb + b], (T, T)) == own
                if b == 2:
                    ok = ok & (lane <= row)
                BIAS[pb, :, b * T:(b + 1) * T] = jnp.where(ok, 0.0, MASKED)

    last = Z + 1

    def guarded(t, lag, f):
        j = t - lag

        @pl.when((j >= 0) & (j < nch))
        def _():
            f(j)

    @pl.loop(0, nch + last + 1)
    def _(t):
        guarded(t, 0, e1)
        for r in range(1, Z):
            guarded(t, r, functools.partial(e2, r=r))
        for r in range(Z):
            guarded(t, r + 1, functools.partial(e3, r=r))
        guarded(t, last, e4)

        @pl.when(t == 1)
        def _():
            prepare()

        guarded(t, 1, teacher)

        def send_out(j):
            o_remote(j).start()
            o_local(j).start()

        guarded(t, last, student)
        guarded(t, last + 1, send_out)

    for pb in range(2):
        EROW[pb] = jnp.sum(jnp.transpose(ACC[pb]), axis=0, keepdims=True)
    e_copy = rc(EROW.at[1 - k], EIN, esend, erecv, at(sib))
    e_copy.start()

    for c in q_copies + bundle(2 + k, at(sib), 0, ktheirs):
        c.wait_send()

    @pl.when(has_next)
    def _():
        for t in range(2):
            for c in bundle(k, at(2 * pair + 2 + t), 1 + t, pl.ds(t * KVh, KVh)):
                c.wait_send()

    @pl.loop(0, nch)
    def _(j):
        for m in range(2):
            p_copy(m, j).wait_send()
        for zz in range(Z):
            @pl.when(has_up & (zz <= z))
            def _():
                up(j, zz).wait_send()

            @pl.when(has_dn & (zz >= z))
            def _():
                dn(j, zz).wait_send()

            yc(j, zz).wait_send()
            xc(j, zz).wait_send()
        o_remote(j).wait_send()
        o_local(j).wait()
        o_wait(j)

    e_copy.wait()
    EROW[k] = (EROW[k] + EIN[...]) * (1.0 / (H * D))
    done = pltpu.make_async_copy(EROW.at[k], err_ref, elsem)
    done.start()
    done.wait()


def fused(n, queries, query_pos, key_values, latent, key_pos, key_up, value_up, segment_ids):
    H, T, D = queries.shape
    C = latent.shape[1]
    PD = key_pos.shape[1]
    KV = key_values.shape[0]
    w = value_up.shape[1]
    Hh, KVh = H // 2, KV // 2
    nch = Hh // CHUNK
    Z = n // 4
    bf, f32 = jnp.bfloat16, jnp.float32
    dma = pltpu.SemaphoreType.DMA
    anywhere = pl.BlockSpec(memory_space=pl.ANY)
    out, err = pl.pallas_call(
        functools.partial(kernel, n),
        out_shape=(
            jax.ShapeDtypeStruct((H, T, D), bf),
            jax.ShapeDtypeStruct((1, T), f32),
        ),
        in_specs=[anywhere] * 8,
        out_specs=(anywhere, anywhere),
        scratch_shapes=[
            pltpu.VMEM((n, 2, Hh, w, D), bf),
            pltpu.VMEM((2, Hh, T, D), bf),
            pltpu.VMEM((2, Hh, PD, T), bf),
            pltpu.VMEM((4 * T, C), bf),
            pltpu.VMEM((PD, 4 * T), bf),
            pltpu.VMEM((4, KVh, 2, T, D), bf),
            pltpu.VMEM((4, 1, T), jnp.int32),
            pltpu.VMEM((2, T, 3 * T), f32),
            pltpu.VMEM((2, Hh, T, D), bf),
            pltpu.VMEM((2, Hh, T, D), bf),
            pltpu.VMEM((2, T, D), f32),
            pltpu.VMEM((2, 1, T), f32),
            pltpu.VMEM((1, T), f32),
            dma((8,)),
            dma((2, nch)), dma((2, nch)),
            dma((2,)), dma((2,)),
            dma((3, 4)), dma((4, 4)),
            dma((1,)), dma((1,)),
            dma((2, nch, Z)), dma((nch, Z)),
            dma((nch, Z)), dma((nch, Z)),
            dma((nch, Z)), dma((nch, Z)),
            dma((nch,)), dma((nch,)), dma((nch,)),
            dma(()), dma(()), dma(()),
        ],
        compiler_params=pltpu.CompilerParams(
            collective_id=0, has_side_effects=True, vmem_limit_bytes=56 * 1024 * 1024),
        name="latent_distill",
    )(
        queries,
        jnp.swapaxes(query_pos, 1, 2),
        key_values,
        latent,
        jnp.swapaxes(key_pos, 0, 1),
        jnp.swapaxes(key_up, 1, 2),
        value_up,
        segment_ids.reshape(1, T),
    )
    return out, err.reshape(T)


def solution(mesh):
    placed = (
        P(None, ("dp", "ctx"), None),
        P(None, ("dp", "ctx"), None),
        P(None, None, ("dp", "ctx"), None),
        P(("dp", "ctx"), None),
        P(("dp", "ctx"), None),
        P(None, None, "ctx"),
        P(None, "ctx", None),
        P(("dp", "ctx")),
    )
    return jax.shard_map(
        functools.partial(fused, mesh.shape["ctx"]),
        mesh=mesh,
        in_specs=placed,
        out_specs=(P(None, ("dp", "ctx"), None), P(("dp", "ctx"))),
        check_vma=False,
    )
```

```python
import functools
import math

import jax
import jax.numpy as jnp
from jax import lax
from jax.experimental import pallas as pl
from jax.experimental.pallas import tpu as pltpu
from jax.sharding import PartitionSpec as P

REACH = 2
MASKED = -1e30
CHUNK = 4
AHEAD = 0
HALO = 0
LOG2E = 1.4426950408889634


def dot(a, b, dims):
    return lax.dot_general(a, b, (dims, ((), ())), preferred_element_type=jnp.float32)


def kernel(
    n,
    q_ref, qp_ref, kv_ref, lat_ref, kp_ref, ku_ref, vu_ref, seg_ref,
    out_ref, err_ref,
    G, QB, QPB, LATB, KPB, KVB, SEGB, BIAS, TO, SO, ACC, EROW, EIN,
    lsem, psend, precv, qsend, qrecv, hsend, hrecv, ssend, srecv,
    zs, zr, ys, yr, xs, xr, ws, wr, osend, orecv, olsem, esend, erecv, elsem,
):
    H, T, D = q_ref.shape
    C = lat_ref.shape[1]
    PD = qp_ref.shape[1]
    KV = kv_ref.shape[0]
    w = ku_ref.shape[1]
    Hh, KVh = H // 2, KV // 2
    hc = CHUNK
    early = hc // 2
    nch = Hh // hc
    per_group = (H // KV) // hc
    Z = n // 4
    i = lax.axis_index("ctx")
    d = lax.axis_index("dp")
    k = i % 2
    y = (i // 2) % 2
    z = i // 4
    x = d % 2
    sib = i + 1 - 2 * k
    ynb = i + 2 - 4 * y
    dx = d + 1 - 2 * x
    pair = i // 2
    has_prev = pair > 0
    has_next = pair < n // 2 - 1
    has_up = z < Z - 1
    has_dn = z > 0

    def at(c, dd=d):
        return {"dp": dd, "ctx": c}

    def rc(src, dst, ss, rs, dev):
        return pltpu.make_async_remote_copy(
            src_ref=src, dst_ref=dst, send_sem=ss, recv_sem=rs,
            device_id=dev, device_id_type=pl.DeviceIdType.MESH)

    bar = pltpu.get_barrier_semaphore()

    def greet(dev):
        pl.semaphore_signal(bar, inc=1, device_id=dev, device_id_type=pl.DeviceIdType.MESH)

    def one_if(c):
        return jnp.where(c, 1, 0).astype(jnp.int32)

    greet(at(sib))
    greet(at(ynb))
    greet(at(i, dx))

    @pl.when(has_up)
    def _():
        greet(at(i + 4))

    @pl.when(has_dn)
    def _():
        greet(at(i - 4))

    @pl.when(has_next)
    def _():
        greet(at(2 * pair + 2))
        greet(at(2 * pair + 3))

    @pl.when(has_prev)
    def _():
        greet(at(2 * pair - 2))
        greet(at(2 * pair - 1))

    mine = pl.ds(k * Hh, Hh)
    theirs = pl.ds((1 - k) * Hh, Hh)
    kmine = pl.ds(k * KVh, KVh)
    ktheirs = pl.ds((1 - k) * KVh, KVh)
    tl = pl.ds(pl.multiple_of((2 + k) * T, T), T)
    locals_ = [
        pltpu.make_async_copy(ku_ref.at[mine], G.at[i, 0], lsem.at[0]),
        pltpu.make_async_copy(vu_ref.at[mine], G.at[i, 1], lsem.at[1]),
        pltpu.make_async_copy(q_ref.at[mine], QB.at[k], lsem.at[2]),
        pltpu.make_async_copy(qp_ref.at[mine], QPB.at[k], lsem.at[3]),
        pltpu.make_async_copy(lat_ref, LATB.at[tl], lsem.at[4]),
        pltpu.make_async_copy(kp_ref, KPB.at[:, tl], lsem.at[5]),
        pltpu.make_async_copy(kv_ref.at[kmine], KVB.at[2 + k], lsem.at[6]),
        pltpu.make_async_copy(seg_ref, SEGB.at[2 + k], lsem.at[7]),
    ]
    for c in locals_:
        c.start()

    @pl.when(jnp.logical_not(has_prev))
    def _():
        LATB[0:2 * T] = jnp.zeros((2 * T, C), LATB.dtype)
        KPB[:, 0:2 * T] = jnp.zeros((PD, 2 * T), KPB.dtype)
        KVB[0:2] = jnp.zeros((2, KVh, 2, T, D), KVB.dtype)
        SEGB[0:2] = jnp.full((2, 1, T), -1, jnp.int32)

    pl.semaphore_wait(
        bar, 3 + one_if(has_up) + one_if(has_dn) + 2 * one_if(has_next) + 2 * one_if(has_prev))

    def p_copy(m, j):
        src = (ku_ref, vu_ref)[m]
        return rc(src.at[pl.ds((1 - k) * Hh + j * hc, hc)], G.at[i, m, pl.ds(j * hc, hc)],
                  psend.at[m, j], precv.at[m, j], at(sib))

    def p_wait(m, j):
        here = G.at[sib, m, pl.ds(j * hc, hc)]
        rc(here, here, psend.at[m, j], precv.at[m, j], at(sib)).wait_recv()

    def bundle(row, target, who, kh):
        col = pl.ds(pl.multiple_of(row * T, T), T)
        return [
            rc(kv_ref.at[kh], KVB.at[row], hsend.at[who, 2], hrecv.at[row, 2], target),
        ] + shared(row, target, who)

    def shared(row, target, who, landed=False):
        col = pl.ds(pl.multiple_of(row * T, T), T)
        dst = (LATB.at[col], KPB.at[:, col], SEGB.at[row])
        src = dst if landed else (lat_ref, kp_ref, seg_ref)
        return [
            rc(a, b, hsend.at[who, e], hrecv.at[row, e], target)
            for a, b, e in zip(src, dst, (0, 1, 3))
        ]

    def to_next():
        first = 2 * pair + 2
        return shared(k, at(first + k), 1) + [
            rc(kv_ref.at[pl.ds(t * KVh, KVh)], KVB.at[k], hsend.at[1 + t, 2],
               hrecv.at[k, 2], at(first + t)) for t in range(2)]

    def forward():
        return shared(k, at(sib), 3, True)

    def bundle_wait(row):
        col = pl.ds(pl.multiple_of(row * T, T), T)
        for idx, ref in enumerate((LATB.at[col], KPB.at[:, col], KVB.at[row], SEGB.at[row])):
            rc(ref, ref, hsend.at[0, idx], hrecv.at[row, idx], at(sib)).wait_recv()

    q_copies = [
        rc(q_ref.at[theirs], QB.at[k], qsend.at[0], qrecv.at[0], at(sib)),
        rc(qp_ref.at[theirs], QPB.at[k], qsend.at[1], qrecv.at[1], at(sib)),
    ]
    for j in range(nch):
        for m in range(2):
            p_copy(m, j).start()
        if j == 0:
            for c in bundle(2 + k, at(sib), 0, ktheirs) + q_copies:
                c.start()

    for c in locals_[:2]:
        c.wait()

    def part(j, zz, xx, first, size):
        return G.at[4 * zz + 2 * y + xx, :, pl.ds(j * hc + first, size)]

    def single(j, zz, yy, xx):
        return G.at[4 * zz + 2 * yy + xx, :, pl.ds(j * hc, hc)]

    class Both:
        def __init__(self, j, zz, way, dev):
            a, b = part(j, zz, x, 0, hc), part(j, zz, 1 - x, 0, early)
            self.copies = [
                rc(a, a, zs.at[way, 0, j, zz], zr.at[0, j, zz], dev),
                rc(b, b, zs.at[way, 1, j, zz], zr.at[1, j, zz], dev),
            ]

        def start(self):
            for c in self.copies:
                c.start()

        def wait_send(self):
            for c in self.copies:
                c.wait_send()

        def wait_recv(self):
            for c in self.copies:
                c.wait_recv()

    def up(j, zz):
        return Both(j, zz, 0, at(i + 4))

    def dn(j, zz):
        return Both(j, zz, 1, at(i - 4))

    def side(j, zz):
        s = part(j, zz, x, early, hc - early)
        return rc(s, s, ws.at[j, zz], wr.at[j, zz], at(i, dx))

    def side_wait(j, zz):
        s = part(j, zz, 1 - x, early, hc - early)
        rc(s, s, ws.at[j, zz], wr.at[j, zz], at(i, dx)).wait_recv()

    def yc(j, zz):
        s = single(j, zz, y, x)
        return rc(s, s, ys.at[j, zz], yr.at[j, zz], at(ynb))

    def yc_wait(j, zz):
        s = single(j, zz, 1 - y, x)
        rc(s, s, ys.at[j, zz], yr.at[j, zz], at(ynb)).wait_recv()

    def xc(j, zz):
        s = single(j, zz, 1 - y, x)
        return rc(s, s, xs.at[j, zz], xr.at[j, zz], at(i, dx))

    def xc_wait(j, zz):
        s = single(j, zz, 1 - y, 1 - x)
        rc(s, s, xs.at[j, zz], xr.at[j, zz], at(i, dx)).wait_recv()

    def e1(j):
        for m in range(2):
            p_wait(m, j)

        @pl.when(has_up)
        def _():
            up(j, z).start()

        @pl.when(has_dn)
        def _():
            dn(j, z).start()

        yc(j, z).start()

    def e2(j, r):
        @pl.when(z - r >= 0)
        def _():
            zz = z - r
            up(j, zz).wait_recv()

            @pl.when(has_up)
            def _():
                up(j, zz).start()

            yc(j, zz).start()
            side(j, zz).start()

        @pl.when(z + r < Z)
        def _():
            zz = z + r
            dn(j, zz).wait_recv()

            @pl.when(has_dn)
            def _():
                dn(j, zz).start()

            yc(j, zz).start()
            side(j, zz).start()

    def e3(j, r):
        if r == 0:
            yc_wait(j, z)
            xc(j, z).start()
            return
        for sign in (-1, 1):
            zz = z + sign * r

            @pl.when((zz >= 0) & (zz < Z))
            def _():
                yc_wait(j, zz)
                xc(j, zz).start()

    def e4(j):
        for zz in range(Z):
            xc_wait(j, zz)

            @pl.when(zz != z)
            def _():
                side_wait(j, zz)

    def probs(s, pb, scale):
        rows = s.shape[0]
        s = (s.reshape(rows // T, T, 3 * T) + BIAS[pb][None]).reshape(rows, 3 * T)
        top = jnp.max(s, axis=-1, keepdims=True)
        e = jnp.exp2((s - top) * (scale * LOG2E))
        return e.astype(jnp.bfloat16), 1.0 / jnp.sum(e, axis=-1, keepdims=True)

    def teacher(j):
        heads = pl.ds(j * hc, hc)
        g = j // per_group
        for pb in range(2):
            q = QB[pb, heads].reshape(hc * T, D)
            keys = KVB[pb:pb + 3, g, 0].reshape(3 * T, D)
            vals = KVB[pb:pb + 3, g, 1].reshape(3 * T, D)
            e, inv = probs(dot(q, keys, ((1,), (1,))), pb, 1.0 / math.sqrt(D))
            o = dot(e, vals, ((1,), (0,))) * inv
            TO[pb, heads] = o.astype(jnp.bfloat16).reshape(hc, T, D)

    def student(j):
        qls = []
        for u in range(hc):
            h = j * hc + u
            q = QB[:, h].reshape(2 * T, D)
            up_k = G[:, 0, h].reshape(C, D)
            qls.append(dot(q, up_k, ((1,), (1,))).astype(jnp.bfloat16))
        los, invs = [], []
        for pb in range(2):
            rows = slice(pb * T, pb * T + 3 * T)
            lat = LATB[rows]
            kp = KPB[:, rows]
            ql = jnp.concatenate([a[pb * T:(pb + 1) * T] for a in qls], 0)
            pos = jnp.concatenate(
                [dot(QPB[pb, j * hc + u], kp, ((0,), (0,))) for u in range(hc)], 0)
            s = dot(ql, lat, ((1,), (1,))) + pos
            e, inv = probs(s, pb, 1.0 / math.sqrt(D + PD))
            los.append(dot(e, lat, ((1,), (0,))).astype(jnp.bfloat16))
            invs.append(inv)
        for u in range(hc):
            h = j * hc + u
            up_v = G[:, 1, h].reshape(C, D)
            cut = slice(u * T, (u + 1) * T)
            lo = jnp.concatenate([los[0][cut], los[1][cut]], 0)
            inv = jnp.concatenate([invs[0][cut], invs[1][cut]], 0)
            so = (dot(lo, up_v, ((1,), (0,))) * inv).astype(jnp.bfloat16).reshape(2, T, D)
            SO[:, h] = so
            diff = so.astype(jnp.float32) - TO[:, h].astype(jnp.float32)
            ACC[...] += diff * diff

    def o_remote(j):
        return rc(SO.at[1 - k, pl.ds(j * hc, hc)], out_ref.at[pl.ds(k * Hh + j * hc, hc)],
                  osend.at[j], orecv.at[j], at(sib))

    def o_wait(j):
        here = out_ref.at[pl.ds((1 - k) * Hh + j * hc, hc)]
        rc(here, here, osend.at[j], orecv.at[j], at(sib)).wait_recv()

    def o_local(j):
        return pltpu.make_async_copy(
            SO.at[k, pl.ds(j * hc, hc)], out_ref.at[pl.ds(k * Hh + j * hc, hc)], olsem.at[j])

    def prepare():
        for c in locals_[2:]:
            c.wait()
        for idx, ref in enumerate((QB.at[1 - k], QPB.at[1 - k])):
            rc(ref, ref, qsend.at[idx], qrecv.at[idx], at(sib)).wait_recv()
        bundle_wait(3 - k)

        @pl.when(has_prev)
        def _():
            bundle_wait(1 - k)
            rc(KVB.at[k], KVB.at[k], hsend.at[0, 2], hrecv.at[k, 2], at(sib)).wait_recv()

        ACC[...] = jnp.zeros_like(ACC)
        row = lax.broadcasted_iota(jnp.int32, (T, T), 0)
        lane = lax.broadcasted_iota(jnp.int32, (T, T), 1)
        for pb in range(2):
            own = jnp.transpose(jnp.broadcast_to(SEGB[2 + pb], (T, T)))
            for b in range(3):
                ok = jnp.broadcast_to(SEGB[pb + b], (T, T)) == own
                if b == 2:
                    ok = ok & (lane <= row)
                BIAS[pb, :, b * T:(b + 1) * T] = jnp.where(ok, 0.0, MASKED)

    ahead = AHEAD
    last = Z + 1 + ahead

    def guarded(t, lag, f):
        j = t - lag

        @pl.when((j >= 0) & (j < nch))
        def _():
            f(j)

    @pl.loop(0, nch + last + 1)
    def _(t):
        guarded(t, 0, e1)
        for r in range(1, Z):
            guarded(t, r + ahead, functools.partial(e2, r=r))
        for r in range(Z):
            guarded(t, r + 1 + ahead, functools.partial(e3, r=r))
        guarded(t, last, e4)

        @pl.when(has_next & (t == HALO))
        def _():
            for c in to_next():
                c.start()

        @pl.when(has_prev & (t == HALO + 1))
        def _():
            for c in shared(k, at(sib), 3, True):
                c.wait_recv()
            for c in forward():
                c.start()

        @pl.when(t == HALO + 2)
        def _():
            prepare()

        guarded(t, HALO + 2, teacher)

        def send_out(j):
            o_remote(j).start()
            o_local(j).start()

        guarded(t, last, student)
        guarded(t, last + 1, send_out)

    for pb in range(2):
        EROW[pb] = jnp.sum(jnp.transpose(ACC[pb]), axis=0, keepdims=True)
    e_copy = rc(EROW.at[1 - k], EIN, esend, erecv, at(sib))
    e_copy.start()

    for c in q_copies + bundle(2 + k, at(sib), 0, ktheirs):
        c.wait_send()

    @pl.when(has_next)
    def _():
        for c in to_next():
            c.wait_send()

    @pl.when(has_prev)
    def _():
        for c in forward():
            c.wait_send()

    @pl.loop(0, nch)
    def _(j):
        for m in range(2):
            p_copy(m, j).wait_send()
        for zz in range(Z):
            @pl.when(has_up & (zz <= z))
            def _():
                up(j, zz).wait_send()

            @pl.when(has_dn & (zz >= z))
            def _():
                dn(j, zz).wait_send()

            yc(j, zz).wait_send()
            xc(j, zz).wait_send()

            @pl.when(zz != z)
            def _():
                side(j, zz).wait_send()

        o_remote(j).wait_send()
        o_local(j).wait()
        o_wait(j)

    e_copy.wait()
    EROW[k] = (EROW[k] + EIN[...]) * (1.0 / (H * D))
    done = pltpu.make_async_copy(EROW.at[k], err_ref, elsem)
    done.start()
    done.wait()


def fused(n, queries, query_pos, key_values, latent, key_pos, key_up, value_up, segment_ids):
    H, T, D = queries.shape
    C = latent.shape[1]
    PD = key_pos.shape[1]
    KV = key_values.shape[0]
    w = value_up.shape[1]
    Hh, KVh = H // 2, KV // 2
    nch = Hh // CHUNK
    Z = n // 4
    bf, f32 = jnp.bfloat16, jnp.float32
    dma = pltpu.SemaphoreType.DMA
    anywhere = pl.BlockSpec(memory_space=pl.ANY)
    out, err = pl.pallas_call(
        functools.partial(kernel, n),
        out_shape=(
            jax.ShapeDtypeStruct((H, T, D), bf),
            jax.ShapeDtypeStruct((1, T), f32),
        ),
        in_specs=[anywhere] * 8,
        out_specs=(anywhere, anywhere),
        scratch_shapes=[
            pltpu.VMEM((n, 2, Hh, w, D), bf),
            pltpu.VMEM((2, Hh, T, D), bf),
            pltpu.VMEM((2, Hh, PD, T), bf),
            pltpu.VMEM((4 * T, C), bf),
            pltpu.VMEM((PD, 4 * T), bf),
            pltpu.VMEM((4, KVh, 2, T, D), bf),
            pltpu.VMEM((4, 1, T), jnp.int32),
            pltpu.VMEM((2, T, 3 * T), f32),
            pltpu.VMEM((2, Hh, T, D), bf),
            pltpu.VMEM((2, Hh, T, D), bf),
            pltpu.VMEM((2, T, D), f32),
            pltpu.VMEM((2, 1, T), f32),
            pltpu.VMEM((1, T), f32),
            dma((8,)),
            dma((2, nch)), dma((2, nch)),
            dma((2,)), dma((2,)),
            dma((4, 4)), dma((4, 4)),
            dma((1,)), dma((1,)),
            dma((2, 2, nch, Z)), dma((2, nch, Z)),
            dma((nch, Z)), dma((nch, Z)),
            dma((nch, Z)), dma((nch, Z)),
            dma((nch, Z)), dma((nch, Z)),
            dma((nch,)), dma((nch,)), dma((nch,)),
            dma(()), dma(()), dma(()),
        ],
        compiler_params=pltpu.CompilerParams(
            collective_id=0, has_side_effects=True, vmem_limit_bytes=56 * 1024 * 1024),
        name="latent_distill",
    )(
        queries,
        jnp.swapaxes(query_pos, 1, 2),
        key_values,
        latent,
        jnp.swapaxes(key_pos, 0, 1),
        jnp.swapaxes(key_up, 1, 2),
        value_up,
        segment_ids.reshape(1, T),
    )
    return out, err.reshape(T)


def solution(mesh):
    placed = (
        P(None, ("dp", "ctx"), None),
        P(None, ("dp", "ctx"), None),
        P(None, None, ("dp", "ctx"), None),
        P(("dp", "ctx"), None),
        P(("dp", "ctx"), None),
        P(None, None, "ctx"),
        P(None, "ctx", None),
        P(("dp", "ctx")),
    )
    return jax.shard_map(
        functools.partial(fused, mesh.shape["ctx"]),
        mesh=mesh,
        in_specs=placed,
        out_specs=(P(None, ("dp", "ctx"), None), P(("dp", "ctx"))),
        check_vma=False,
    )
```

```python
import functools
import math

import jax
import jax.numpy as jnp
from jax import lax
from jax.experimental import pallas as pl
from jax.experimental.pallas import tpu as pltpu
from jax.sharding import PartitionSpec as P

REACH = 2
MASKED = -1e30
CHUNK = 4
AHEAD = 0
HALO = 0
LOG2E = 1.4426950408889634


def dot(a, b, dims):
    return lax.dot_general(a, b, (dims, ((), ())), preferred_element_type=jnp.float32)


def kernel(
    n,
    q_ref, qp_ref, kv_ref, lat_ref, kp_ref, ku_ref, vu_ref, seg_ref,
    out_ref, err_ref,
    G, QB, QPB, LATB, KPB, KVB, SEGB, BIAS, TO, SO, ACC, EROW, EIN,
    lsem, psend, precv, qsend, qrecv, hsend, hrecv, ssend, srecv,
    zs, zr, ys, yr, xs, xr, ws, wr, osend, orecv, olsem, esend, erecv, elsem,
):
    H, T, D = q_ref.shape
    C = lat_ref.shape[1]
    PD = qp_ref.shape[1]
    KV = kv_ref.shape[0]
    w = ku_ref.shape[1]
    Hh, KVh = H // 2, KV // 2
    hc = CHUNK
    early = hc // 2
    nch = Hh // hc
    per_group = (H // KV) // hc
    Z = n // 4
    i = lax.axis_index("ctx")
    d = lax.axis_index("dp")
    k = i % 2
    y = (i // 2) % 2
    z = i // 4
    x = d % 2
    sib = i + 1 - 2 * k
    ynb = i + 2 - 4 * y
    dx = d + 1 - 2 * x
    pair = i // 2
    has_prev = pair > 0
    has_next = pair < n // 2 - 1
    has_up = z < Z - 1
    has_dn = z > 0

    def at(c, dd=d):
        return {"dp": dd, "ctx": c}

    def rc(src, dst, ss, rs, dev):
        return pltpu.make_async_remote_copy(
            src_ref=src, dst_ref=dst, send_sem=ss, recv_sem=rs,
            device_id=dev, device_id_type=pl.DeviceIdType.MESH)

    bar = pltpu.get_barrier_semaphore()

    def greet(dev):
        pl.semaphore_signal(bar, inc=1, device_id=dev, device_id_type=pl.DeviceIdType.MESH)

    def one_if(c):
        return jnp.where(c, 1, 0).astype(jnp.int32)

    greet(at(sib))
    greet(at(ynb))
    greet(at(i, dx))

    @pl.when(has_up)
    def _():
        greet(at(i + 4))

    @pl.when(has_dn)
    def _():
        greet(at(i - 4))

    @pl.when(has_next)
    def _():
        greet(at(2 * pair + 2))
        greet(at(2 * pair + 3))

    @pl.when(has_prev)
    def _():
        greet(at(2 * pair - 2))
        greet(at(2 * pair - 1))

    mine = pl.ds(k * Hh, Hh)
    theirs = pl.ds((1 - k) * Hh, Hh)
    kmine = pl.ds(k * KVh, KVh)
    ktheirs = pl.ds((1 - k) * KVh, KVh)
    tl = pl.ds(pl.multiple_of((2 + k) * T, T), T)
    locals_ = [
        pltpu.make_async_copy(ku_ref.at[mine], G.at[i, 0], lsem.at[0]),
        pltpu.make_async_copy(vu_ref.at[mine], G.at[i, 1], lsem.at[1]),
        pltpu.make_async_copy(q_ref.at[mine], QB.at[k], lsem.at[2]),
        pltpu.make_async_copy(qp_ref.at[mine], QPB.at[k], lsem.at[3]),
        pltpu.make_async_copy(lat_ref, LATB.at[tl], lsem.at[4]),
        pltpu.make_async_copy(kp_ref, KPB.at[:, tl], lsem.at[5]),
        pltpu.make_async_copy(kv_ref.at[kmine], KVB.at[2 + k], lsem.at[6]),
        pltpu.make_async_copy(seg_ref, SEGB.at[2 + k], lsem.at[7]),
    ]
    for c in locals_:
        c.start()

    @pl.when(jnp.logical_not(has_prev))
    def _():
        LATB[0:2 * T] = jnp.zeros((2 * T, C), LATB.dtype)
        KPB[:, 0:2 * T] = jnp.zeros((PD, 2 * T), KPB.dtype)
        KVB[0:2] = jnp.zeros((2, KVh, 2, T, D), KVB.dtype)
        SEGB[0:2] = jnp.full((2, 1, T), -1, jnp.int32)

    pl.semaphore_wait(
        bar, 3 + one_if(has_up) + one_if(has_dn) + 2 * one_if(has_next) + 2 * one_if(has_prev))

    def p_copy(m, j):
        src = (ku_ref, vu_ref)[m]
        return rc(src.at[pl.ds((1 - k) * Hh + j * hc, hc)], G.at[i, m, pl.ds(j * hc, hc)],
                  psend.at[m, j], precv.at[m, j], at(sib))

    def p_wait(m, j):
        here = G.at[sib, m, pl.ds(j * hc, hc)]
        rc(here, here, psend.at[m, j], precv.at[m, j], at(sib)).wait_recv()

    def bundle(row, target, who, kh):
        col = pl.ds(pl.multiple_of(row * T, T), T)
        return [
            rc(kv_ref.at[kh], KVB.at[row], hsend.at[who, 2], hrecv.at[row, 2], target),
        ] + shared(row, target, who)

    def shared(row, target, who, landed=False):
        col = pl.ds(pl.multiple_of(row * T, T), T)
        dst = (LATB.at[col], KPB.at[:, col], SEGB.at[row])
        src = dst if landed else (lat_ref, kp_ref, seg_ref)
        return [
            rc(a, b, hsend.at[who, e], hrecv.at[row, e], target)
            for a, b, e in zip(src, dst, (0, 1, 3))
        ]

    def to_next():
        first = 2 * pair + 2
        return shared(k, at(first + k), 1) + [
            rc(kv_ref.at[pl.ds(t * KVh, KVh)], KVB.at[k], hsend.at[1 + t, 2],
               hrecv.at[k, 2], at(first + t)) for t in range(2)]

    def forward():
        return shared(k, at(sib), 3, True)

    def bundle_wait(row):
        col = pl.ds(pl.multiple_of(row * T, T), T)
        for idx, ref in enumerate((LATB.at[col], KPB.at[:, col], KVB.at[row], SEGB.at[row])):
            rc(ref, ref, hsend.at[0, idx], hrecv.at[row, idx], at(sib)).wait_recv()

    q_copies = [
        rc(q_ref.at[theirs], QB.at[k], qsend.at[0], qrecv.at[0], at(sib)),
        rc(qp_ref.at[theirs], QPB.at[k], qsend.at[1], qrecv.at[1], at(sib)),
    ]
    for j in range(nch):
        for m in range(2):
            p_copy(m, j).start()
        if j == 0:
            for c in bundle(2 + k, at(sib), 0, ktheirs) + q_copies:
                c.start()

    for c in locals_[:2]:
        c.wait()

    def part(j, zz, xx, first, size):
        return G.at[4 * zz + 2 * y + xx, :, pl.ds(j * hc + first, size)]

    def single(j, zz, yy, xx):
        return G.at[4 * zz + 2 * yy + xx, :, pl.ds(j * hc, hc)]

    class Both:
        def __init__(self, j, zz, way, dev):
            a, b = part(j, zz, x, 0, hc), part(j, zz, 1 - x, 0, early)
            self.copies = [
                rc(a, a, zs.at[way, 0, j, zz], zr.at[0, j, zz], dev),
                rc(b, b, zs.at[way, 1, j, zz], zr.at[1, j, zz], dev),
            ]

        def start(self):
            for c in self.copies:
                c.start()

        def wait_send(self):
            for c in self.copies:
                c.wait_send()

        def wait_recv(self):
            for c in self.copies:
                c.wait_recv()

    def up(j, zz):
        return Both(j, zz, 0, at(i + 4))

    def dn(j, zz):
        return Both(j, zz, 1, at(i - 4))

    def side(j, zz):
        s = part(j, zz, x, early, hc - early)
        return rc(s, s, ws.at[j, zz], wr.at[j, zz], at(i, dx))

    def side_wait(j, zz):
        s = part(j, zz, 1 - x, early, hc - early)
        rc(s, s, ws.at[j, zz], wr.at[j, zz], at(i, dx)).wait_recv()

    def yc(j, zz):
        s = single(j, zz, y, x)
        return rc(s, s, ys.at[j, zz], yr.at[j, zz], at(ynb))

    def yc_wait(j, zz):
        s = single(j, zz, 1 - y, x)
        rc(s, s, ys.at[j, zz], yr.at[j, zz], at(ynb)).wait_recv()

    def xc(j, zz):
        s = single(j, zz, 1 - y, x)
        return rc(s, s, xs.at[j, zz], xr.at[j, zz], at(i, dx))

    def xc_wait(j, zz):
        s = single(j, zz, 1 - y, 1 - x)
        rc(s, s, xs.at[j, zz], xr.at[j, zz], at(i, dx)).wait_recv()

    def e1(j):
        for m in range(2):
            p_wait(m, j)

        @pl.when(has_up)
        def _():
            up(j, z).start()

        @pl.when(has_dn)
        def _():
            dn(j, z).start()

        yc(j, z).start()

    def e2(j, r):
        @pl.when(z - r >= 0)
        def _():
            zz = z - r
            up(j, zz).wait_recv()

            @pl.when(has_up)
            def _():
                up(j, zz).start()

            yc(j, zz).start()
            side(j, zz).start()

        @pl.when(z + r < Z)
        def _():
            zz = z + r
            dn(j, zz).wait_recv()

            @pl.when(has_dn)
            def _():
                dn(j, zz).start()

            yc(j, zz).start()
            side(j, zz).start()

    def e3(j, r):
        if r == 0:
            yc_wait(j, z)
            xc(j, z).start()
            return
        for sign in (-1, 1):
            zz = z + sign * r

            @pl.when((zz >= 0) & (zz < Z))
            def _():
                yc_wait(j, zz)
                xc(j, zz).start()

    def e4(j):
        for zz in range(Z):
            xc_wait(j, zz)

            @pl.when(zz != z)
            def _():
                side_wait(j, zz)

    def probs(s, pb, scale):
        rows = s.shape[0]
        s = (s.reshape(rows // T, T, 3 * T) + BIAS[pb][None]).reshape(rows, 3 * T)
        top = jnp.max(s, axis=-1, keepdims=True)
        e = jnp.exp2((s - top) * (scale * LOG2E))
        return e.astype(jnp.bfloat16), 1.0 / jnp.sum(e, axis=-1, keepdims=True)

    def teacher(j):
        heads = pl.ds(j * hc, hc)
        g = j // per_group
        for pb in range(2):
            q = QB[pb, heads].reshape(hc * T, D)
            keys = KVB[pb:pb + 3, g, 0].reshape(3 * T, D)
            vals = KVB[pb:pb + 3, g, 1].reshape(3 * T, D)
            e, inv = probs(dot(q, keys, ((1,), (1,))), pb, 1.0 / math.sqrt(D))
            o = dot(e, vals, ((1,), (0,))) * inv
            TO[pb, heads] = o.astype(jnp.bfloat16).reshape(hc, T, D)

    def student(j):
        qls = []
        for u in range(hc):
            h = j * hc + u
            q = QB[:, h].reshape(2 * T, D)
            up_k = G[:, 0, h].reshape(C, D)
            qls.append(dot(q, up_k, ((1,), (1,))).astype(jnp.bfloat16))
        los, invs = [], []
        for pb in range(2):
            rows = slice(pb * T, pb * T + 3 * T)
            lat = LATB[rows]
            kp = KPB[:, rows]
            ql = jnp.concatenate([a[pb * T:(pb + 1) * T] for a in qls], 0)
            pos = jnp.concatenate(
                [dot(QPB[pb, j * hc + u], kp, ((0,), (0,))) for u in range(hc)], 0)
            s = dot(ql, lat, ((1,), (1,))) + pos
            e, inv = probs(s, pb, 1.0 / math.sqrt(D + PD))
            los.append(dot(e, lat, ((1,), (0,))).astype(jnp.bfloat16))
            invs.append(inv)
        for u in range(hc):
            h = j * hc + u
            up_v = G[:, 1, h].reshape(C, D)
            cut = slice(u * T, (u + 1) * T)
            lo = jnp.concatenate([los[0][cut], los[1][cut]], 0)
            inv = jnp.concatenate([invs[0][cut], invs[1][cut]], 0)
            so = (dot(lo, up_v, ((1,), (0,))) * inv).astype(jnp.bfloat16).reshape(2, T, D)
            SO[:, h] = so
            diff = so.astype(jnp.float32) - TO[:, h].astype(jnp.float32)
            ACC[...] += diff * diff

    def o_remote(j):
        return rc(SO.at[1 - k, pl.ds(j * hc, hc)], out_ref.at[pl.ds(k * Hh + j * hc, hc)],
                  osend.at[j], orecv.at[j], at(sib))

    def o_wait(j):
        here = out_ref.at[pl.ds((1 - k) * Hh + j * hc, hc)]
        rc(here, here, osend.at[j], orecv.at[j], at(sib)).wait_recv()

    def o_local(j):
        return pltpu.make_async_copy(
            SO.at[k, pl.ds(j * hc, hc)], out_ref.at[pl.ds(k * Hh + j * hc, hc)], olsem.at[j])

    def prepare():
        for c in locals_[2:]:
            c.wait()
        for idx, ref in enumerate((QB.at[1 - k], QPB.at[1 - k])):
            rc(ref, ref, qsend.at[idx], qrecv.at[idx], at(sib)).wait_recv()
        bundle_wait(3 - k)

        @pl.when(has_prev)
        def _():
            bundle_wait(1 - k)
            rc(KVB.at[k], KVB.at[k], hsend.at[0, 2], hrecv.at[k, 2], at(sib)).wait_recv()

        ACC[...] = jnp.zeros_like(ACC)
        row = lax.broadcasted_iota(jnp.int32, (T, T), 0)
        lane = lax.broadcasted_iota(jnp.int32, (T, T), 1)
        for pb in range(2):
            own = jnp.transpose(jnp.broadcast_to(SEGB[2 + pb], (T, T)))
            for b in range(3):
                ok = jnp.broadcast_to(SEGB[pb + b], (T, T)) == own
                if b == 2:
                    ok = ok & (lane <= row)
                BIAS[pb, :, b * T:(b + 1) * T] = jnp.where(ok, 0.0, MASKED)

    ahead = AHEAD
    last = Z + 1 + ahead

    def guarded(t, lag, f):
        j = t - lag

        @pl.when((j >= 0) & (j < nch))
        def _():
            f(j)

    @pl.loop(0, nch + last + 1)
    def _(t):
        guarded(t, 0, e1)
        for r in range(Z):
            guarded(t, r + 1 + ahead, functools.partial(e3, r=r))
        for r in range(1, Z):
            guarded(t, r + ahead, functools.partial(e2, r=r))
        guarded(t, last, e4)

        @pl.when(has_next & (t == HALO))
        def _():
            for c in to_next():
                c.start()

        @pl.when(has_prev & (t == HALO + 1))
        def _():
            for c in shared(k, at(sib), 3, True):
                c.wait_recv()
            for c in forward():
                c.start()

        @pl.when(t == HALO + 2)
        def _():
            prepare()

        guarded(t, HALO + 2, teacher)

        def send_out(j):
            o_remote(j).start()
            o_local(j).start()

        guarded(t, last, student)
        guarded(t, last + 1, send_out)

    for pb in range(2):
        EROW[pb] = jnp.sum(jnp.transpose(ACC[pb]), axis=0, keepdims=True)
    e_copy = rc(EROW.at[1 - k], EIN, esend, erecv, at(sib))
    e_copy.start()

    for c in q_copies + bundle(2 + k, at(sib), 0, ktheirs):
        c.wait_send()

    @pl.when(has_next)
    def _():
        for c in to_next():
            c.wait_send()

    @pl.when(has_prev)
    def _():
        for c in forward():
            c.wait_send()

    @pl.loop(0, nch)
    def _(j):
        for m in range(2):
            p_copy(m, j).wait_send()
        for zz in range(Z):
            @pl.when(has_up & (zz <= z))
            def _():
                up(j, zz).wait_send()

            @pl.when(has_dn & (zz >= z))
            def _():
                dn(j, zz).wait_send()

            yc(j, zz).wait_send()
            xc(j, zz).wait_send()

            @pl.when(zz != z)
            def _():
                side(j, zz).wait_send()

        o_remote(j).wait_send()
        o_local(j).wait()
        o_wait(j)

    e_copy.wait()
    EROW[k] = (EROW[k] + EIN[...]) * (1.0 / (H * D))
    done = pltpu.make_async_copy(EROW.at[k], err_ref, elsem)
    done.start()
    done.wait()


def fused(n, queries, query_pos, key_values, latent, key_pos, key_up, value_up, segment_ids):
    H, T, D = queries.shape
    C = latent.shape[1]
    PD = key_pos.shape[1]
    KV = key_values.shape[0]
    w = value_up.shape[1]
    Hh, KVh = H // 2, KV // 2
    nch = Hh // CHUNK
    Z = n // 4
    bf, f32 = jnp.bfloat16, jnp.float32
    dma = pltpu.SemaphoreType.DMA
    anywhere = pl.BlockSpec(memory_space=pl.ANY)
    out, err = pl.pallas_call(
        functools.partial(kernel, n),
        out_shape=(
            jax.ShapeDtypeStruct((H, T, D), bf),
            jax.ShapeDtypeStruct((1, T), f32),
        ),
        in_specs=[anywhere] * 8,
        out_specs=(anywhere, anywhere),
        scratch_shapes=[
            pltpu.VMEM((n, 2, Hh, w, D), bf),
            pltpu.VMEM((2, Hh, T, D), bf),
            pltpu.VMEM((2, Hh, PD, T), bf),
            pltpu.VMEM((4 * T, C), bf),
            pltpu.VMEM((PD, 4 * T), bf),
            pltpu.VMEM((4, KVh, 2, T, D), bf),
            pltpu.VMEM((4, 1, T), jnp.int32),
            pltpu.VMEM((2, T, 3 * T), f32),
            pltpu.VMEM((2, Hh, T, D), bf),
            pltpu.VMEM((2, Hh, T, D), bf),
            pltpu.VMEM((2, T, D), f32),
            pltpu.VMEM((2, 1, T), f32),
            pltpu.VMEM((1, T), f32),
            dma((8,)),
            dma((2, nch)), dma((2, nch)),
            dma((2,)), dma((2,)),
            dma((4, 4)), dma((4, 4)),
            dma((1,)), dma((1,)),
            dma((2, 2, nch, Z)), dma((2, nch, Z)),
            dma((nch, Z)), dma((nch, Z)),
            dma((nch, Z)), dma((nch, Z)),
            dma((nch, Z)), dma((nch, Z)),
            dma((nch,)), dma((nch,)), dma((nch,)),
            dma(()), dma(()), dma(()),
        ],
        compiler_params=pltpu.CompilerParams(
            collective_id=0, has_side_effects=True, vmem_limit_bytes=56 * 1024 * 1024),
        name="latent_distill",
    )(
        queries,
        jnp.swapaxes(query_pos, 1, 2),
        key_values,
        latent,
        jnp.swapaxes(key_pos, 0, 1),
        jnp.swapaxes(key_up, 1, 2),
        value_up,
        segment_ids.reshape(1, T),
    )
    return out, err.reshape(T)


def solution(mesh):
    placed = (
        P(None, ("dp", "ctx"), None),
        P(None, ("dp", "ctx"), None),
        P(None, None, ("dp", "ctx"), None),
        P(("dp", "ctx"), None),
        P(("dp", "ctx"), None),
        P(None, None, "ctx"),
        P(None, "ctx", None),
        P(("dp", "ctx")),
    )
    return jax.shard_map(
        functools.partial(fused, mesh.shape["ctx"]),
        mesh=mesh,
        in_specs=placed,
        out_specs=(P(None, ("dp", "ctx"), None), P(("dp", "ctx"))),
        check_vma=False,
    )
```

```python
import functools
import math

import jax
import jax.numpy as jnp
from jax import lax
from jax.experimental import pallas as pl
from jax.experimental.pallas import tpu as pltpu
from jax.sharding import PartitionSpec as P

REACH = 2
MASKED = -1e30
CHUNK = 4
AHEAD = 0
HALO = 0
LOG2E = 1.4426950408889634


def dot(a, b, dims):
    return lax.dot_general(a, b, (dims, ((), ())), preferred_element_type=jnp.float32)


def kernel(
    n,
    q_ref, qp_ref, kv_ref, lat_ref, kp_ref, ku_ref, vu_ref, seg_ref,
    out_ref, err_ref,
    G, QB, QPB, LATB, KPB, KVB, SEGB, BIAS, TO, SO, ACC, EROW, EIN,
    lsem, psend, precv, qsend, qrecv, hsend, hrecv, ssend, srecv,
    zs, zr, ys, yr, xs, xr, ws, wr, osend, orecv, olsem, esend, erecv, elsem,
):
    H, T, D = q_ref.shape
    C = lat_ref.shape[1]
    PD = qp_ref.shape[1]
    KV = kv_ref.shape[0]
    w = ku_ref.shape[1]
    Hh, KVh = H // 2, KV // 2
    hc = CHUNK
    early = hc // 2
    nch = Hh // hc
    per_group = (H // KV) // hc
    Z = n // 4
    i = lax.axis_index("ctx")
    d = lax.axis_index("dp")
    k = i % 2
    y = (i // 2) % 2
    z = i // 4
    x = d % 2
    sib = i + 1 - 2 * k
    ynb = i + 2 - 4 * y
    dx = d + 1 - 2 * x
    pair = i // 2
    has_prev = pair > 0
    has_next = pair < n // 2 - 1
    has_up = z < Z - 1
    has_dn = z > 0

    def at(c, dd=d):
        return {"dp": dd, "ctx": c}

    def rc(src, dst, ss, rs, dev):
        return pltpu.make_async_remote_copy(
            src_ref=src, dst_ref=dst, send_sem=ss, recv_sem=rs,
            device_id=dev, device_id_type=pl.DeviceIdType.MESH)

    bar = pltpu.get_barrier_semaphore()

    def greet(dev):
        pl.semaphore_signal(bar, inc=1, device_id=dev, device_id_type=pl.DeviceIdType.MESH)

    def one_if(c):
        return jnp.where(c, 1, 0).astype(jnp.int32)

    greet(at(sib))
    greet(at(ynb))
    greet(at(i, dx))

    @pl.when(has_up)
    def _():
        greet(at(i + 4))

    @pl.when(has_dn)
    def _():
        greet(at(i - 4))

    @pl.when(has_next)
    def _():
        greet(at(2 * pair + 2))
        greet(at(2 * pair + 3))

    @pl.when(has_prev)
    def _():
        greet(at(2 * pair - 2))
        greet(at(2 * pair - 1))

    mine = pl.ds(k * Hh, Hh)
    theirs = pl.ds((1 - k) * Hh, Hh)
    kmine = pl.ds(k * KVh, KVh)
    ktheirs = pl.ds((1 - k) * KVh, KVh)
    tl = pl.ds(pl.multiple_of((2 + k) * T, T), T)
    locals_ = [
        pltpu.make_async_copy(ku_ref.at[mine], G.at[i, 0], lsem.at[0]),
        pltpu.make_async_copy(vu_ref.at[mine], G.at[i, 1], lsem.at[1]),
        pltpu.make_async_copy(q_ref.at[mine], QB.at[k], lsem.at[2]),
        pltpu.make_async_copy(qp_ref.at[mine], QPB.at[k], lsem.at[3]),
        pltpu.make_async_copy(lat_ref, LATB.at[tl], lsem.at[4]),
        pltpu.make_async_copy(kp_ref, KPB.at[:, tl], lsem.at[5]),
        pltpu.make_async_copy(kv_ref.at[kmine], KVB.at[2 + k], lsem.at[6]),
        pltpu.make_async_copy(seg_ref, SEGB.at[2 + k], lsem.at[7]),
    ]
    for c in locals_:
        c.start()

    @pl.when(jnp.logical_not(has_prev))
    def _():
        LATB[0:2 * T] = jnp.zeros((2 * T, C), LATB.dtype)
        KPB[:, 0:2 * T] = jnp.zeros((PD, 2 * T), KPB.dtype)
        KVB[0:2] = jnp.zeros((2, KVh, 2, T, D), KVB.dtype)
        SEGB[0:2] = jnp.full((2, 1, T), -1, jnp.int32)

    pl.semaphore_wait(
        bar, 3 + one_if(has_up) + one_if(has_dn) + 2 * one_if(has_next) + 2 * one_if(has_prev))

    def p_copy(m, j):
        src = (ku_ref, vu_ref)[m]
        return rc(src.at[pl.ds((1 - k) * Hh + j * hc, hc)], G.at[i, m, pl.ds(j * hc, hc)],
                  psend.at[m, j], precv.at[m, j], at(sib))

    def p_wait(m, j):
        here = G.at[sib, m, pl.ds(j * hc, hc)]
        rc(here, here, psend.at[m, j], precv.at[m, j], at(sib)).wait_recv()

    def bundle(row, target, who, kh):
        col = pl.ds(pl.multiple_of(row * T, T), T)
        return [
            rc(kv_ref.at[kh], KVB.at[row], hsend.at[who, 2], hrecv.at[row, 2], target),
        ] + shared(row, target, who)

    def shared(row, target, who, landed=False):
        col = pl.ds(pl.multiple_of(row * T, T), T)
        dst = (LATB.at[col], KPB.at[:, col], SEGB.at[row])
        src = dst if landed else (lat_ref, kp_ref, seg_ref)
        return [
            rc(a, b, hsend.at[who, e], hrecv.at[row, e], target)
            for a, b, e in zip(src, dst, (0, 1, 3))
        ]

    def to_next():
        first = 2 * pair + 2
        return shared(k, at(first + k), 1) + [
            rc(kv_ref.at[pl.ds(t * KVh, KVh)], KVB.at[k], hsend.at[1 + t, 2],
               hrecv.at[k, 2], at(first + t)) for t in range(2)]

    def forward():
        return shared(k, at(sib), 3, True)

    def bundle_wait(row):
        col = pl.ds(pl.multiple_of(row * T, T), T)
        for idx, ref in enumerate((LATB.at[col], KPB.at[:, col], KVB.at[row], SEGB.at[row])):
            rc(ref, ref, hsend.at[0, idx], hrecv.at[row, idx], at(sib)).wait_recv()

    q_copies = [
        rc(q_ref.at[theirs], QB.at[k], qsend.at[0], qrecv.at[0], at(sib)),
        rc(qp_ref.at[theirs], QPB.at[k], qsend.at[1], qrecv.at[1], at(sib)),
    ]
    for j in range(nch):
        for m in range(2):
            p_copy(m, j).start()
        if j == 0:
            for c in bundle(2 + k, at(sib), 0, ktheirs) + q_copies:
                c.start()

    for c in locals_[:2]:
        c.wait()

    def part(j, zz, xx, first, size):
        return G.at[4 * zz + 2 * y + xx, :, pl.ds(j * hc + first, size)]

    def single(j, zz, yy, xx):
        return G.at[4 * zz + 2 * yy + xx, :, pl.ds(j * hc, hc)]

    class Both:
        def __init__(self, j, zz, way, dev):
            a, b = part(j, zz, x, 0, hc), part(j, zz, 1 - x, 0, early)
            self.copies = [
                rc(a, a, zs.at[way, 0, j, zz], zr.at[0, j, zz], dev),
                rc(b, b, zs.at[way, 1, j, zz], zr.at[1, j, zz], dev),
            ]

        def start(self):
            for c in self.copies:
                c.start()

        def wait_send(self):
            for c in self.copies:
                c.wait_send()

        def wait_recv(self):
            for c in self.copies:
                c.wait_recv()

    def up(j, zz):
        return Both(j, zz, 0, at(i + 4))

    def dn(j, zz):
        return Both(j, zz, 1, at(i - 4))

    def side(j, zz):
        s = part(j, zz, x, early, hc - early)
        return rc(s, s, ws.at[j, zz], wr.at[j, zz], at(i, dx))

    def side_wait(j, zz):
        s = part(j, zz, 1 - x, early, hc - early)
        rc(s, s, ws.at[j, zz], wr.at[j, zz], at(i, dx)).wait_recv()

    def yc(j, zz):
        s = single(j, zz, y, x)
        return rc(s, s, ys.at[j, zz], yr.at[j, zz], at(ynb))

    def yc_wait(j, zz):
        s = single(j, zz, 1 - y, x)
        rc(s, s, ys.at[j, zz], yr.at[j, zz], at(ynb)).wait_recv()

    def xc(j, zz):
        s = single(j, zz, 1 - y, x)
        return rc(s, s, xs.at[j, zz], xr.at[j, zz], at(i, dx))

    def xc_wait(j, zz):
        s = single(j, zz, 1 - y, 1 - x)
        rc(s, s, xs.at[j, zz], xr.at[j, zz], at(i, dx)).wait_recv()

    def e1(j):
        for m in range(2):
            p_wait(m, j)

        @pl.when(has_up)
        def _():
            up(j, z).start()

        @pl.when(has_dn)
        def _():
            dn(j, z).start()

        yc(j, z).start()

    def e2(j, r):
        @pl.when(z - r >= 0)
        def _():
            zz = z - r
            up(j, zz).wait_recv()

            @pl.when(has_up)
            def _():
                up(j, zz).start()

            yc(j, zz).start()
            side(j, zz).start()

        @pl.when(z + r < Z)
        def _():
            zz = z + r
            dn(j, zz).wait_recv()

            @pl.when(has_dn)
            def _():
                dn(j, zz).start()

            yc(j, zz).start()
            side(j, zz).start()

    def e3(j, r):
        if r == 0:
            yc_wait(j, z)
            xc(j, z).start()
            return
        for sign in (-1, 1):
            zz = z + sign * r

            @pl.when((zz >= 0) & (zz < Z))
            def _():
                yc_wait(j, zz)
                xc(j, zz).start()

    def e4(j):
        for zz in range(Z):
            xc_wait(j, zz)

            @pl.when(zz != z)
            def _():
                side_wait(j, zz)

    def probs(s, pb, scale):
        rows = s.shape[0]
        s = (s.reshape(rows // T, T, 3 * T) + BIAS[pb][None]).reshape(rows, 3 * T)
        top = jnp.max(s, axis=-1, keepdims=True)
        e = jnp.exp2((s - top) * (scale * LOG2E))
        return e.astype(jnp.bfloat16), 1.0 / jnp.sum(e, axis=-1, keepdims=True)

    def teacher(j):
        heads = pl.ds(j * hc, hc)
        g = j // per_group
        for pb in range(2):
            q = QB[pb, heads].reshape(hc * T, D)
            keys = KVB[pb:pb + 3, g, 0].reshape(3 * T, D)
            vals = KVB[pb:pb + 3, g, 1].reshape(3 * T, D)
            e, inv = probs(dot(q, keys, ((1,), (1,))), pb, 1.0 / math.sqrt(D))
            o = dot(e, vals, ((1,), (0,))) * inv
            TO[pb, heads] = o.astype(jnp.bfloat16).reshape(hc, T, D)

    def student(j):
        qls = []
        for u in range(hc):
            h = j * hc + u
            q = QB[:, h].reshape(2 * T, D)
            up_k = G[:, 0, h].reshape(C, D)
            qls.append(dot(q, up_k, ((1,), (1,))).astype(jnp.bfloat16))
        los, invs = [], []
        for pb in range(2):
            rows = slice(pb * T, pb * T + 3 * T)
            lat = LATB[rows]
            kp = KPB[:, rows]
            ql = jnp.concatenate([a[pb * T:(pb + 1) * T] for a in qls], 0)
            pos = jnp.concatenate(
                [dot(QPB[pb, j * hc + u], kp, ((0,), (0,))) for u in range(hc)], 0)
            s = dot(ql, lat, ((1,), (1,))) + pos
            e, inv = probs(s, pb, 1.0 / math.sqrt(D + PD))
            los.append(dot(e, lat, ((1,), (0,))).astype(jnp.bfloat16))
            invs.append(inv)
        for u in range(hc):
            h = j * hc + u
            up_v = G[:, 1, h].reshape(C, D)
            cut = slice(u * T, (u + 1) * T)
            lo = jnp.concatenate([los[0][cut], los[1][cut]], 0)
            inv = jnp.concatenate([invs[0][cut], invs[1][cut]], 0)
            so = (dot(lo, up_v, ((1,), (0,))) * inv).astype(jnp.bfloat16).reshape(2, T, D)
            SO[:, h] = so
            diff = so.astype(jnp.float32) - TO[:, h].astype(jnp.float32)
            ACC[...] += diff * diff

    def o_remote(j):
        return rc(SO.at[1 - k, pl.ds(j * hc, hc)], out_ref.at[pl.ds(k * Hh + j * hc, hc)],
                  osend.at[j], orecv.at[j], at(sib))

    def o_wait(j):
        here = out_ref.at[pl.ds((1 - k) * Hh + j * hc, hc)]
        rc(here, here, osend.at[j], orecv.at[j], at(sib)).wait_recv()

    def o_local(j):
        return pltpu.make_async_copy(
            SO.at[k, pl.ds(j * hc, hc)], out_ref.at[pl.ds(k * Hh + j * hc, hc)], olsem.at[j])

    def prepare():
        for c in locals_[2:]:
            c.wait()
        for idx, ref in enumerate((QB.at[1 - k], QPB.at[1 - k])):
            rc(ref, ref, qsend.at[idx], qrecv.at[idx], at(sib)).wait_recv()
        bundle_wait(3 - k)

        @pl.when(has_prev)
        def _():
            bundle_wait(1 - k)
            rc(KVB.at[k], KVB.at[k], hsend.at[0, 2], hrecv.at[k, 2], at(sib)).wait_recv()

        ACC[...] = jnp.zeros_like(ACC)
        row = lax.broadcasted_iota(jnp.int32, (T, T), 0)
        lane = lax.broadcasted_iota(jnp.int32, (T, T), 1)
        for pb in range(2):
            own = jnp.transpose(jnp.broadcast_to(SEGB[2 + pb], (T, T)))
            for b in range(3):
                ok = jnp.broadcast_to(SEGB[pb + b], (T, T)) == own
                if b == 2:
                    ok = ok & (lane <= row)
                BIAS[pb, :, b * T:(b + 1) * T] = jnp.where(ok, 0.0, MASKED)

    ahead = AHEAD
    last = Z + 1 + ahead

    def guarded(t, lag, f):
        j = t - lag

        @pl.when((j >= 0) & (j < nch))
        def _():
            f(j)

    @pl.loop(0, nch + last + 1)
    def _(t):
        guarded(t, 0, e1)
        for r in range(Z):
            guarded(t, r + 1 + ahead, functools.partial(e3, r=r))
        for r in range(Z - 1, 0, -1):
            guarded(t, r + ahead, functools.partial(e2, r=r))
        guarded(t, last, e4)

        @pl.when(has_next & (t == HALO))
        def _():
            for c in to_next():
                c.start()

        @pl.when(has_prev & (t == HALO + 1))
        def _():
            for c in shared(k, at(sib), 3, True):
                c.wait_recv()
            for c in forward():
                c.start()

        @pl.when(t == HALO + 2)
        def _():
            prepare()

        guarded(t, HALO + 2, teacher)

        def send_out(j):
            o_remote(j).start()
            o_local(j).start()

        guarded(t, last, student)
        guarded(t, last + 1, send_out)

    for pb in range(2):
        EROW[pb] = jnp.sum(jnp.transpose(ACC[pb]), axis=0, keepdims=True)
    e_copy = rc(EROW.at[1 - k], EIN, esend, erecv, at(sib))
    e_copy.start()

    for c in q_copies + bundle(2 + k, at(sib), 0, ktheirs):
        c.wait_send()

    @pl.when(has_next)
    def _():
        for c in to_next():
            c.wait_send()

    @pl.when(has_prev)
    def _():
        for c in forward():
            c.wait_send()

    @pl.loop(0, nch)
    def _(j):
        for m in range(2):
            p_copy(m, j).wait_send()
        for zz in range(Z):
            @pl.when(has_up & (zz <= z))
            def _():
                up(j, zz).wait_send()

            @pl.when(has_dn & (zz >= z))
            def _():
                dn(j, zz).wait_send()

            yc(j, zz).wait_send()
            xc(j, zz).wait_send()

            @pl.when(zz != z)
            def _():
                side(j, zz).wait_send()

        o_remote(j).wait_send()
        o_local(j).wait()
        o_wait(j)

    e_copy.wait()
    EROW[k] = (EROW[k] + EIN[...]) * (1.0 / (H * D))
    done = pltpu.make_async_copy(EROW.at[k], err_ref, elsem)
    done.start()
    done.wait()


def fused(n, queries, query_pos, key_values, latent, key_pos, key_up, value_up, segment_ids):
    H, T, D = queries.shape
    C = latent.shape[1]
    PD = key_pos.shape[1]
    KV = key_values.shape[0]
    w = value_up.shape[1]
    Hh, KVh = H // 2, KV // 2
    nch = Hh // CHUNK
    Z = n // 4
    bf, f32 = jnp.bfloat16, jnp.float32
    dma = pltpu.SemaphoreType.DMA
    anywhere = pl.BlockSpec(memory_space=pl.ANY)
    out, err = pl.pallas_call(
        functools.partial(kernel, n),
        out_shape=(
            jax.ShapeDtypeStruct((H, T, D), bf),
            jax.ShapeDtypeStruct((1, T), f32),
        ),
        in_specs=[anywhere] * 8,
        out_specs=(anywhere, anywhere),
        scratch_shapes=[
            pltpu.VMEM((n, 2, Hh, w, D), bf),
            pltpu.VMEM((2, Hh, T, D), bf),
            pltpu.VMEM((2, Hh, PD, T), bf),
            pltpu.VMEM((4 * T, C), bf),
            pltpu.VMEM((PD, 4 * T), bf),
            pltpu.VMEM((4, KVh, 2, T, D), bf),
            pltpu.VMEM((4, 1, T), jnp.int32),
            pltpu.VMEM((2, T, 3 * T), f32),
            pltpu.VMEM((2, Hh, T, D), bf),
            pltpu.VMEM((2, Hh, T, D), bf),
            pltpu.VMEM((2, T, D), f32),
            pltpu.VMEM((2, 1, T), f32),
            pltpu.VMEM((1, T), f32),
            dma((8,)),
            dma((2, nch)), dma((2, nch)),
            dma((2,)), dma((2,)),
            dma((4, 4)), dma((4, 4)),
            dma((1,)), dma((1,)),
            dma((2, 2, nch, Z)), dma((2, nch, Z)),
            dma((nch, Z)), dma((nch, Z)),
            dma((nch, Z)), dma((nch, Z)),
            dma((nch, Z)), dma((nch, Z)),
            dma((nch,)), dma((nch,)), dma((nch,)),
            dma(()), dma(()), dma(()),
        ],
        compiler_params=pltpu.CompilerParams(
            collective_id=0, has_side_effects=True, vmem_limit_bytes=56 * 1024 * 1024),
        name="latent_distill",
    )(
        queries,
        jnp.swapaxes(query_pos, 1, 2),
        key_values,
        latent,
        jnp.swapaxes(key_pos, 0, 1),
        jnp.swapaxes(key_up, 1, 2),
        value_up,
        segment_ids.reshape(1, T),
    )
    return out, err.reshape(T)


def solution(mesh):
    placed = (
        P(None, ("dp", "ctx"), None),
        P(None, ("dp", "ctx"), None),
        P(None, None, ("dp", "ctx"), None),
        P(("dp", "ctx"), None),
        P(("dp", "ctx"), None),
        P(None, None, "ctx"),
        P(None, "ctx", None),
        P(("dp", "ctx")),
    )
    return jax.shard_map(
        functools.partial(fused, mesh.shape["ctx"]),
        mesh=mesh,
        in_specs=placed,
        out_specs=(P(None, ("dp", "ctx"), None), P(("dp", "ctx"))),
        check_vma=False,
    )
```
